256 devices in a mesh: ctx: 64 (over z, x, core), ch: 4 (over y).
Axes of the slice: x: 4, y: 4, z: 8, core: 2. Of those that a mesh axis runs over, the one named last changes fastest.
Arguments:
- queries: bfloat16 [8192, 8192], P('ctx', 'ch'), may hold values from -6 to 6
- keys: bfloat16 [8192, 8192], P('ctx', 'ch'), may hold values from -6 to 6
- values: bfloat16 [8192, 8192], P('ctx', 'ch'), may hold values from -6 to 6
- short_taps: float32 [3, 7, 8192], P(None, None, 'ch'), may hold values from -2 to 2
- residues: float32 [512, 16], P('ch'), may hold values from -1.5 to 1.5
- decay_rate: float32 [512, 16], P('ch'), may hold values from 2.4414063e-05 to 0.03125
- out_gain: float32 [8192], P('ch'), may hold values from 0.5 to 1.5
- doc_lengths: int32 [16], replicated, may hold values from 1 to 4096, 8192 in all
- upstream: bfloat16 [8192, 8192], P('ctx', 'ch'), may hold values from -6 to 6
Outputs:
- mixed_out: bfloat16 [8192, 8192], P('ctx', 'ch')
- d_queries: bfloat16 [8192, 8192], P('ctx', 'ch')
- d_keys: bfloat16 [8192, 8192], P('ctx', 'ch')
- d_values: bfloat16 [8192, 8192], P('ctx', 'ch')
- d_taps: float32 [3, 7, 8192], P(None, None, 'ch')
- d_residues: float32 [512, 16], P('ch')
- d_rate: float32 [512, 16], P('ch')
- d_gain: float32 [8192], P('ch')
The draws below stay inside these ranges and needn't reach their ends.
Inputs may be any that keep to these rules, and one draw needn't show every extreme that they name: `doc_lengths`: the lengths sum to 8192, and one document is exactly 4096 positions long.
All inputs are finite; a program needn't handle non-finite values.
Results may differ from the reference program's by a relative error of at most 0.01.
Values may be sent and summed in bfloat16 or wider, within the bound.
A program may use at most 192 MiB of HBM per device.

```python
import math
import jax
import jax.numpy as jnp
import numpy as np
from jax import lax

D = 8192
GROUP = 16
MODES = 16
TAPS = 7
NDOC = 16
TOK_DEV = 128
TOKENS = 8192
NGROUPS = 512


def levels(rng, dims, shards, low, top_value):
    loudness, own = 1.0, jax.random.fold_in(rng, 6)
    for dim, parts in shards:
        heights = jnp.exp(jax.random.uniform(jax.random.fold_in(own, dim), (parts,), jnp.float32, low / len(shards), top_value / len(shards)))
        loudness = loudness * jnp.repeat(heights, dims[dim] // parts).reshape([-1 if axis == dim else 1 for axis in range(len(dims))])
    return loudness


def profile(number_of, total, bound, slope):
    weights = [(1 << 20) // math.isqrt(rank ** slope) + 1 for rank in range(2, number_of + 1)]
    rest, counts = total - bound - (number_of - 1), [1] * (number_of - 1)
    while rest > 0:
        movable = [i for i in range(number_of - 1) if counts[i] < bound]
        mass, left = sum([weights[i] for i in movable]), rest
        for i in movable:
            addition = min(bound - counts[i], max(1, left * weights[i] // mass), rest)
            counts[i] = counts[i] + addition
            rest = rest - addition
    return np.array([bound] + counts)


def ragged_sizes(rng, number_of, total, reach, lean):
    if number_of == 2:
        one = jax.random.randint(rng, (), max(1, total - reach), min(reach, total - 1) + 1)
        return jnp.stack([one, total - one])
    sizes = jnp.asarray(profile(number_of, total, reach, lean), jnp.int32)
    pairs = (number_of - 1) // 2
    giver, receiver = sizes[1:1 + 2 * pairs:2], sizes[2:2 + 2 * pairs:2]
    margin = jnp.minimum(giver - 1, reach - receiver)
    moved = jax.random.randint(jax.random.fold_in(rng, 1), (pairs,), 0, 1 << 20) % (margin + 1)
    sizes = sizes.at[1:1 + 2 * pairs:2].set(giver - moved).at[2:2 + 2 * pairs:2].set(receiver + moved)
    return sizes[jax.random.permutation(jax.random.fold_in(rng, 2), number_of)]


def scatter_about(stream_key, extent, width, limit, cuts=(), held_as=jnp.bfloat16):
    entries = width * jax.random.normal(stream_key, extent, jnp.float32)
    if cuts:
        entries = entries * levels(stream_key, extent, cuts, -0.22, 0.18)
    return jnp.clip(entries, -limit, limit).astype(held_as)


def setup_inputs(seed: int = 0) -> dict:
    streams_of = jax.random.split(jax.random.key(seed), 10)
    queries = scatter_about(streams_of[0], (TOKENS, D), 1.0, 6.0, ((0, 64), (1, 4)))
    keys = scatter_about(streams_of[1], (TOKENS, D), 1.0, 6.0, ((0, 64), (1, 4)))
    values = scatter_about(streams_of[2], (TOKENS, D), 1.0, 6.0, ((0, 64), (1, 4)))
    short_taps = scatter_about(streams_of[3], (3, TAPS, D), TAPS ** -0.5, 2.0, ((2, 4),), jnp.float32)
    residues = scatter_about(streams_of[4], (NGROUPS, MODES), MODES ** -0.5, 1.5, ((0, 4),), jnp.float32)
    decay_rate = jnp.clip(jnp.exp(math.log(0.03125) - 7.1546153 * jax.random.uniform(streams_of[5], (NGROUPS, MODES), jnp.float32) ** levels(streams_of[5], (NGROUPS, MODES), ((0, 4),), -0.2, 0.2)), 2.441406286379788e-05, 0.03125)
    out_gain = jnp.clip(1.0 + 0.1 * jax.random.normal(streams_of[6], (D,), jnp.float32), 0.5, 1.5)
    doc_lengths = ragged_sizes(streams_of[7], NDOC, TOKENS, TOKENS // 2, 2).astype(jnp.int32)
    upstream = scatter_about(streams_of[8], (TOKENS, D), 1.0, 6.0, ((0, 64), (1, 4)))
    return dict(queries=queries, keys=keys, values=values, short_taps=short_taps, residues=residues, decay_rate=decay_rate, out_gain=out_gain, doc_lengths=doc_lengths, upstream=upstream)


epsilon = 1e-06
highest = lax.Precision.HIGHEST
entry_limit = 2097152

def doc_index(doc_lengths, positions):
    starts = jnp.cumsum(doc_lengths) - doc_lengths
    return lax.optimization_barrier(jnp.sum((starts[None, :] <= positions[:, None]).astype(jnp.int32), axis=1)) - 1

def spread_groups(per_group):
    return jnp.repeat(per_group.T, GROUP, axis=1)

def mode_gain(decay_rate):
    return jnp.sqrt(-jnp.expm1(-2.0 * decay_rate))

def local_part(mixed, doc_ids, prev_doc, residues, decay_rate):
    row_count, channels = mixed.shape
    group_count = channels // GROUP
    mode_count = decay_rate.shape[1]
    lag_steps = jnp.arange(row_count, dtype=jnp.float32)
    weighted = residues * mode_gain(decay_rate)
    filter_rows = jnp.einsum('gn,gnd->gd', weighted, jnp.exp(-decay_rate[:, :, None] * lag_steps[None, None, :]), precision=highest)
    row_index = jnp.arange(row_count, dtype=jnp.int32)
    lag_table = row_index[:, None] - row_index[None, :]
    causal_mask = (lag_table >= 0) & (doc_ids[:, None] == doc_ids[None, :])
    safe_lags = jnp.maximum(lag_table, 0)
    per_step = group_count
    while per_step % 2 == 0 and per_step * row_count * row_count > entry_limit:
        per_step = per_step // 2
    step_count = group_count // per_step
    mixed_cols = mixed.T.reshape(group_count, GROUP, row_count)
    table_steps = filter_rows.reshape(step_count, per_step, row_count)
    mixed_steps = mixed_cols.reshape(step_count, per_step, GROUP, row_count)

    def toeplitz_block(pieces):
        table_part, mixed_part = pieces
        toeplitz = jnp.where(causal_mask[None, :, :], table_part[:, safe_lags], 0.0)
        return jnp.einsum('gts,gis->git', toeplitz, mixed_part, precision=highest)
    outputs = lax.map(jax.checkpoint(toeplitz_block), (table_steps, mixed_steps))
    within = outputs.reshape(channels, row_count).T
    same_last = (doc_ids == doc_ids[row_count - 1]).astype(jnp.float32)
    backward_decay = jnp.exp(-decay_rate[:, :, None] * (row_count - 1.0 - lag_steps)[None, None, :]) * same_last[None, None, :]
    end_state = jnp.einsum('gns,gis->ngi', backward_decay, mixed_cols, precision=highest).reshape(mode_count, channels)
    through = (doc_ids[row_count - 1] == prev_doc).astype(jnp.float32)
    pass_decay = spread_groups(jnp.exp(-decay_rate * row_count) * through)
    return (within, pass_decay, end_state)

def tail_part(doc_ids, prev_doc, residues, decay_rate, state):
    row_count = doc_ids.shape[0]
    mode_count, channels = state.shape
    group_count = channels // GROUP
    lag_steps = jnp.arange(row_count, dtype=jnp.float32)
    weighted = residues * mode_gain(decay_rate)
    carried_mask = (doc_ids == prev_doc).astype(jnp.float32)
    decays = weighted[:, :, None] * jnp.exp(-decay_rate[:, :, None] * (lag_steps + 1.0)[None, None, :]) * carried_mask[None, None, :]
    state_cols = state.reshape(mode_count, group_count, GROUP).transpose(1, 2, 0)
    carried_cols = jnp.einsum('gnt,gin->git', decays, state_cols, precision=highest)
    return carried_cols.reshape(channels, row_count).T

def full_conv(mixed, doc_ids, residues, decay_rate, block):
    row_count, channels = mixed.shape
    step_count = row_count // block
    mode_count = decay_rate.shape[1]
    block_ends = doc_ids[block - 1::block][:-1]
    prev_docs = jnp.concatenate([jnp.full((1,), -1, jnp.int32), block_ends.astype(jnp.int32)])

    def advance(state, pieces):
        mixed_part, doc_part, prev_doc = pieces
        within, pass_decay, end_state = local_part(mixed_part, doc_part, prev_doc, residues, decay_rate)
        carried_part = tail_part(doc_part, prev_doc, residues, decay_rate, state)
        return (pass_decay * state + end_state, within + carried_part)
    start_state = jnp.zeros((mode_count, channels), jnp.float32)
    _, outputs = lax.scan(jax.checkpoint(advance), start_state, (mixed.reshape(step_count, block, channels), doc_ids.reshape(step_count, block), prev_docs))
    return outputs.reshape(row_count, channels)

def short_forward(extended, ext_docs, taps):
    row_count = extended.shape[0] - (TAPS - 1)
    doc_here = ext_docs[TAPS - 1:]
    summed = jnp.zeros((row_count, extended.shape[1]), jnp.float32)
    for lag in range(TAPS):
        begin = TAPS - 1 - lag
        same_doc = (ext_docs[begin:begin + row_count] == doc_here).astype(jnp.float32)
        summed = summed + taps[lag][None, :] * extended[begin:begin + row_count] * same_doc[:, None]
    return summed

def reference(queries, keys, values, short_taps, residues, decay_rate, out_gain, doc_lengths, upstream):
    doc_ids = doc_index(doc_lengths, jnp.arange(TOKENS, dtype=jnp.int32))
    pad_docs = jnp.concatenate([jnp.full((TAPS - 1,), -1, jnp.int32), doc_ids.astype(jnp.int32)])
    padding = jnp.zeros((TAPS - 1, D), jnp.float32)

    def forward(query_in, key_in, value_in, taps, resid_in, rate_in, gain_in):
        qs = short_forward(jnp.concatenate([padding, query_in]), pad_docs, taps[0])
        ks = short_forward(jnp.concatenate([padding, key_in]), pad_docs, taps[1])
        vs = short_forward(jnp.concatenate([padding, value_in]), pad_docs, taps[2])
        conv = full_conv(ks * vs, doc_ids, resid_in, rate_in, TOK_DEV)
        gated = qs * conv
        inverse = lax.rsqrt(lax.optimization_barrier(jnp.sum(gated * gated, axis=1)) / D + epsilon)
        return gated * inverse[:, None] * gain_in
    out_full, backward = jax.vjp(forward, queries.astype(jnp.float32), keys.astype(jnp.float32), values.astype(jnp.float32), short_taps, residues, decay_rate, out_gain)
    grads = backward(upstream.astype(jnp.float32))
    return (out_full.astype(jnp.bfloat16), grads[0].astype(jnp.bfloat16), grads[1].astype(jnp.bfloat16), grads[2].astype(jnp.bfloat16), grads[3], grads[4], grads[5], grads[6])
```

```python
import functools

import jax
import jax.numpy as jnp
from jax import lax
from jax.experimental import pallas as pl
from jax.experimental.pallas import tpu as pltpu
from jax.sharding import PartitionSpec as P

D = 8192
TOKENS = 8192
GROUP = 16
MODES = 16
TAPS = 7
ROWS = 128
LANES = 128
TILES = 16
PLANE = 8
LEVELS = 8
CHIPS_Y = 4
EXT = 8
epsilon = 1e-06
f32 = jnp.float32
bf16 = jnp.bfloat16
MESH = pl.DeviceIdType.MESH


def doc_index(starts, positions):
    return jnp.sum((starts[None, :] <= positions[:, None]).astype(jnp.int32), axis=1) - 1


def aligned(index, size):
    return pl.ds(pl.multiple_of(index * size, size), size)


def kernel(
    scal,
    q_hbm,
    k_hbm,
    v_hbm,
    u_hbm,
    taps,
    gain,
    docs,
    lam_lane,
    mode_lane,
    rate_lane,
    lam_rows,
    w_rows,
    out_ref,
    dq_ref,
    dk_ref,
    dv_ref,
    dtaps_ref,
    dres_ref,
    drate_ref,
    dgain_ref,
    qbuf,
    kbuf,
    vbuf,
    ubuf,
    qhalo,
    khalo,
    vhalo,
    qext,
    kext,
    vext,
    qs_ref,
    ks_ref,
    vs_ref,
    conv_ref,
    mix16,
    dconv16,
    mix_s,
    win_s,
    dc_s,
    dm_s,
    saved,
    mask,
    a0,
    a1,
    d0,
    d1,
    e_n,
    w_n,
    gq,
    gk,
    gv,
    sg0,
    s2,
    sg2,
    dw_acc,
    de_acc,
    part_a,
    part_b,
    ysend,
    yrecv,
    f_send,
    f_recv,
    f_tot,
    f_zrecv,
    f_back,
    f_full,
    b_send,
    b_recv,
    b_tot,
    b_zrecv,
    b_back,
    b_full,
    e_send,
    e_recv,
    e_tot,
    e_zrecv,
    e_full,
    l_send,
    l_recv,
    l_tot,
    l_zrecv,
    l_full,
    load_sem,
    halo_s,
    halo_r,
    y_s,
    y_r,
    send_sem,
    recv_sem,
):
    me = lax.axis_index("ctx")
    cy = lax.axis_index("ch")
    level = me // PLANE
    spot = lax.rem(me, PLANE)
    nodes = PLANE * LEVELS
    after = lax.rem(me + 1, nodes)
    before = lax.rem(me + nodes - 1, nodes)

    def in_plane(step):
        return lax.rem(spot + step, PLANE)

    def on_level(step):
        return lax.rem(level + step, LEVELS)

    barrier = pltpu.get_barrier_semaphore()
    for step in range(1, PLANE):
        pl.semaphore_signal(
            barrier, inc=1, device_id={"ctx": level * PLANE + in_plane(step)}, device_id_type=MESH
        )
    for step in range(1, LEVELS):
        pl.semaphore_signal(
            barrier, inc=1, device_id={"ctx": on_level(step) * PLANE + spot}, device_id_type=MESH
        )
    for step in range(1, CHIPS_Y):
        pl.semaphore_signal(
            barrier, inc=1, device_id={"ch": lax.rem(cy + step, CHIPS_Y)}, device_id_type=MESH
        )
    for other in (before, after):
        pl.semaphore_signal(barrier, inc=1, device_id={"ctx": other}, device_id_type=MESH)

    loads = [
        pltpu.make_async_copy(source, target, load_sem.at[i])
        for i, (source, target) in enumerate(
            ((k_hbm, kbuf), (v_hbm, vbuf), (q_hbm, qbuf), (u_hbm, ubuf))
        )
    ]
    for load in loads:
        load.start()

    here = docs[EXT : EXT + ROWS + EXT, :]
    for lag in range(1, TAPS):
        same = docs[EXT - lag : EXT - lag + ROWS + EXT, :] == here
        mask[lag] = jnp.where(same, 1.0, 0.0)
    first_mask = jnp.where(docs[EXT : EXT + ROWS, :] == docs[EXT - 1 : EXT, :], 1.0, 0.0)
    last_mask = jnp.where(
        docs[EXT : EXT + ROWS, :] == docs[EXT + ROWS - 1 : EXT + ROWS, :], 1.0, 0.0
    )
    part_a[...] = first_mask
    part_b[...] = last_mask
    row_number = lax.broadcasted_iota(jnp.int32, (ROWS, LANES), 0).astype(f32)
    on_group = lax.broadcasted_iota(jnp.int32, (8, MODES, LANES), 0) == (
        lax.broadcasted_iota(jnp.int32, (8, MODES, LANES), 2) // GROUP
    )

    @pl.loop(0, TILES)
    def _(tile):
        cols = aligned(tile, LANES)
        lam = lam_lane[pl.ds(tile, 1), :]
        ahead = jnp.exp(-lam * (row_number + 1.0)) * part_a[...]
        behind = jnp.exp(-lam * (ROWS - 1.0 - row_number)) * part_b[...]
        a0[:, cols] = ahead.astype(bf16)
        d0[:, cols] = behind.astype(bf16)
        a1[:, cols] = (ahead * (row_number + 1.0)).astype(bf16)
        d1[:, cols] = (behind * (ROWS - 1.0 - row_number)).astype(bf16)

    @pl.loop(0, MODES)
    def _(mode):
        e_n[mode] = jnp.exp(-lam_rows[pl.ds(mode, TILES, stride=MODES), :])
        w_n[mode] = w_rows[pl.ds(mode, TILES, stride=MODES), :]

    pl.semaphore_wait(barrier, PLANE - 1 + LEVELS - 1 + CHIPS_Y - 1 + 2)

    halos = [
        pltpu.make_async_remote_copy(
            src_ref=source.at[pl.ds(ROWS - 16, 16)],
            dst_ref=target,
            send_sem=halo_s.at[i],
            recv_sem=halo_r.at[i],
            device_id={"ctx": after},
            device_id_type=MESH,
        )
        for i, (source, target) in enumerate(((k_hbm, khalo), (v_hbm, vhalo), (q_hbm, qhalo)))
    ]
    for halo in halos:
        halo.start()

    def widen(buf, halo, ext, cols):
        ext[EXT : EXT + ROWS, cols] = buf[:, cols].astype(f32)
        ext[0:EXT, cols] = halo[:, cols].astype(f32)[8:16]

    def feature(ext, which, cols):
        total = taps[which, 0:1, cols] * ext[EXT : EXT + ROWS, cols]
        for lag in range(1, TAPS):
            shifted = ext[EXT - lag : EXT - lag + ROWS, cols] * mask[lag, 0:ROWS, :]
            total = total + taps[which, lag : lag + 1, cols] * shifted
        return total

    def per_mode(left, right):
        blocks = lax.dot_general(left, right, (((0,), (0,)), ((), ())), preferred_element_type=f32)
        return jnp.sum(jnp.where(on_group, blocks.reshape(8, MODES, LANES), 0.0), axis=0)

    def spread(state):
        wide = jnp.broadcast_to(state[None], (8, MODES, LANES))
        return jnp.where(on_group, wide, 0.0).reshape(8 * MODES, LANES).astype(bf16)

    def sent_in_plane(base, source, target, step):
        other = in_plane(step)
        return source(other), target, other

    def plane_copies(base, source, target, chunk):
        out, back = [], []
        for step in range(1, PLANE):
            other = in_plane(step)
            device = level * PLANE + other
            src = source(other)
            out.append(
                pltpu.make_async_remote_copy(
                    src_ref=src,
                    dst_ref=target(spot),
                    send_sem=send_sem.at[base, other],
                    recv_sem=recv_sem.at[base, spot],
                    device_id={"ctx": device},
                    device_id_type=MESH,
                )
            )
            back.append(
                pltpu.make_async_remote_copy(
                    src_ref=src,
                    dst_ref=target(other),
                    send_sem=send_sem.at[base, other],
                    recv_sem=recv_sem.at[base, other],
                    device_id={"ctx": device},
                    device_id_type=MESH,
                )
            )
        return out, back

    def level_copies(base, source, target):
        out, back = [], []
        for step in range(1, LEVELS):
            other = on_level(step)
            device = other * PLANE + spot
            for kept, slot in ((out, level), (back, other)):
                kept.append(
                    pltpu.make_async_remote_copy(
                        src_ref=source,
                        dst_ref=target.at[slot],
                        send_sem=send_sem.at[base, other],
                        recv_sem=recv_sem.at[base, slot],
                        device_id={"ctx": device},
                        device_id_type=MESH,
                    )
                )
        return out, back

    def begin(copies):
        for copy in copies[0]:
            copy.start()

    def finish(copies):
        for copy in copies[1]:
            copy.wait()

    def exchange(base, send, recv, tot, zrecv, back, full, chunk):
        first = plane_copies(base, lambda o: send.at[aligned(o, chunk)], lambda s: recv.at[s], chunk)
        second = level_copies(base + 1, tot, zrecv)
        if back is None:
            third = plane_copies(
                base + 2,
                lambda o: full.at[aligned(spot, chunk)],
                lambda s: full.at[aligned(s, chunk)],
                chunk,
            )
        else:
            third = plane_copies(
                base + 2, lambda o: back.at[o], lambda s: full.at[aligned(s, chunk)], chunk
            )
        return first, second, third

    forward = exchange(0, f_send, f_recv, f_tot, f_zrecv, f_back, f_full, 32)
    reverse = exchange(3, b_send, b_recv, b_tot, b_zrecv, b_back, b_full, 32)
    early = exchange(6, e_send, e_recv, e_tot, e_zrecv, None, e_full, 16)
    late = exchange(9, l_send, l_recv, l_tot, l_zrecv, None, l_full, 32)

    own_rows = aligned(spot, 32)

    def plane_flag(position):
        return scal[ROWS + position]

    def level_flag(position):
        return scal[ROWS + PLANE + position]

    loads[0].wait()
    loads[1].wait()
    halos[0].wait()
    halos[1].wait()

    @pl.loop(0, TILES)
    def _(tile):
        cols = aligned(tile, LANES)
        widen(kbuf, khalo, kext, cols)
        widen(vbuf, vhalo, vext, cols)
        ks = feature(kext, 1, cols)
        vs = feature(vext, 2, cols)
        mixed = ks * vs
        ks_ref[:, cols] = ks
        vs_ref[:, cols] = vs
        mix_s[pl.ds(tile, ROWS, stride=TILES), :] = mixed
        mix16[:, cols] = mixed.astype(bf16)
        f_send[aligned(tile, MODES), :] = per_mode(d0[:, cols], mixed.astype(bf16))

    begin(forward[0])
    loads[2].wait()
    loads[3].wait()
    halos[2].wait()

    @pl.loop(0, TILES)
    def _(tile):
        cols = aligned(tile, LANES)
        widen(qbuf, qhalo, qext, cols)
        qs_ref[:, cols] = feature(qext, 0, cols)

    step_decay = jnp.exp(-lam_rows[own_rows, :] * float(ROWS))
    level_decay = jnp.exp(-lam_rows[own_rows, :] * float(ROWS * PLANE))

    finish(forward[0])
    f_recv[spot] = f_send[own_rows, :]
    total = f_recv[0]
    for position in range(1, PLANE):
        total = plane_flag(position) * step_decay * total + f_recv[position]
    f_tot[...] = total
    begin(forward[1])

    def scan_forward(half):
        rows = slice(half * 8, half * 8 + 8)
        decay = e_n[:, rows, :]
        weight = w_n[:, rows, :]

        def turn(t, state):
            place = pl.ds(pl.multiple_of(t * TILES + half * 8, 8), 8)
            state = state * (decay * scal[t]) + mix_s[place, :][None]
            saved[half, t] = state
            win_s[place, :] = jnp.sum(state * weight, axis=0)
            return state

        lax.fori_loop(0, ROWS, turn, jnp.zeros((MODES, 8, LANES), f32))

    scan_forward(0)
    scan_forward(1)

    finish(forward[1])
    f_zrecv[level] = f_tot[...]
    enter = jnp.zeros_like(total)
    for position in range(LEVELS - 1):
        longer = level_flag(position) * level_decay * enter + f_zrecv[position]
        enter = jnp.where(position < level, longer, enter)
    f_back[0] = enter
    for position in range(PLANE - 1):
        enter = plane_flag(position) * step_decay * enter + f_recv[position]
        f_back[position + 1] = enter
    begin(forward[2])
    f_full[own_rows, :] = f_back[spot]

    @pl.loop(0, TILES)
    def _(tile):
        cols = aligned(tile, LANES)
        s2[aligned(tile, MODES), :] = per_mode(d1[:, cols], mix16[:, cols])

    finish(forward[2])

    part_a[...] = jnp.zeros_like(part_a)
    part_b[...] = jnp.zeros_like(part_b)

    @pl.loop(0, TILES)
    def _(tile):
        cols = aligned(tile, LANES)
        rows = aligned(tile, MODES)
        carried = jnp.dot(
            a0[:, cols], spread(f_full[rows, :] * w_rows[rows, :]), preferred_element_type=f32
        )
        conv = win_s[pl.ds(tile, ROWS, stride=TILES), :] + carried
        conv_ref[:, cols] = conv
        gated = qs_ref[:, cols] * conv
        part_a[...] += gated * gated
        part_b[...] += ubuf[:, cols].astype(f32) * gain[0:1, cols] * gated

    squares = jnp.sum(part_a[...].T, axis=0, keepdims=True)
    inner = jnp.sum(part_b[...].T, axis=0, keepdims=True)
    upper = lax.broadcasted_iota(jnp.int32, (8, LANES), 0) == 0
    ysend[...] = jnp.where(
        upper, jnp.broadcast_to(squares, (8, LANES)), jnp.broadcast_to(inner, (8, LANES))
    )
    y_out, y_back = [], []
    for step in range(1, CHIPS_Y):
        other = lax.rem(cy + step, CHIPS_Y)
        for kept, slot in ((y_out, cy), (y_back, other)):
            kept.append(
                pltpu.make_async_remote_copy(
                    src_ref=ysend,
                    dst_ref=yrecv.at[slot],
                    send_sem=y_s.at[other],
                    recv_sem=y_r.at[slot],
                    device_id={"ch": other},
                    device_id_type=MESH,
                )
            )
    begin((y_out, y_back))
    finish((y_out, y_back))
    yrecv[cy] = ysend[...]
    sums = yrecv[0] + yrecv[1] + yrecv[2] + yrecv[3]
    inv_row = lax.rsqrt(sums[0:1] / D + epsilon)
    pull_row = inv_row * inv_row * inv_row * sums[1:2] / D
    part_a[...] = jnp.broadcast_to(inv_row, (ROWS, LANES)).T
    part_b[...] = jnp.broadcast_to(pull_row, (ROWS, LANES)).T

    @pl.loop(0, TILES)
    def _(tile):
        cols = aligned(tile, LANES)
        rows = aligned(tile, MODES)
        qs = qs_ref[:, cols]
        conv = conv_ref[:, cols]
        inverse = part_a[...]
        up = ubuf[:, cols].astype(f32)
        scale = gain[0:1, cols]
        gated = qs * conv
        d_gated = inverse * (up * scale) - gated * part_b[...]
        normed = gated * inverse
        d_conv = d_gated * qs
        out_ref[:, cols] = (normed * scale).astype(bf16)
        gq[0:ROWS, cols] = d_gated * conv
        dc_s[pl.ds(tile, ROWS, stride=TILES), :] = d_conv
        dconv16[:, cols] = d_conv.astype(bf16)
        local = per_mode(a0[:, cols], d_conv.astype(bf16))
        sg0[rows, :] = local
        b_send[rows, :] = local * w_rows[rows, :]
        e_send[pl.ds(tile * 8 + 7, 1), :] = jnp.sum(up * normed, axis=0, keepdims=True)

    begin(reverse[0])

    def halo_back(index, ref):
        return pltpu.make_async_remote_copy(
            src_ref=ref.at[pl.ds(0, 8)],
            dst_ref=ref.at[pl.ds(ROWS, 8)],
            send_sem=halo_s.at[3 + index],
            recv_sem=halo_r.at[3 + index],
            device_id={"ctx": before},
            device_id_type=MESH,
        )

    q_back, k_back, v_back = halo_back(0, gq), halo_back(1, gk), halo_back(2, gv)
    q_back.start()

    def tap_rows(grad, ext, cols):
        rows = []
        here = grad[0:ROWS, cols]
        for lag in range(TAPS):
            product = here * ext[EXT - lag : EXT - lag + ROWS, cols]
            if lag:
                product = product * mask[lag, 0:ROWS, :]
            rows.append(jnp.sum(product, axis=0, keepdims=True))
        return rows

    def feature_back(grad, which, cols):
        total = taps[which, 0:1, cols] * grad[0:ROWS, cols]
        for lag in range(1, TAPS):
            shifted = grad[lag : lag + ROWS, cols] * mask[lag, lag : lag + ROWS, :]
            total = total + taps[which, lag : lag + 1, cols] * shifted
        return total.astype(bf16)

    @pl.loop(0, TILES)
    def _(tile):
        cols = aligned(tile, LANES)
        for lag, row in enumerate(tap_rows(gq, qext, cols)):
            e_send[pl.ds(tile * 8 + lag, 1), :] = row

    begin(early[0])

    finish(reverse[0])
    b_recv[spot] = b_send[own_rows, :]
    total = b_recv[PLANE - 1]
    for position in range(PLANE - 2, -1, -1):
        total = b_recv[position] + plane_flag(position) * step_decay * total
    b_tot[...] = total
    begin(reverse[1])

    def scan_reverse(half, part):
        rows = slice(half * 8, half * 8 + 8)
        modes = slice(part * 8, part * 8 + 8)
        decay = e_n[modes, rows, :]
        weight = w_n[modes, rows, :]
        zero = jnp.zeros((8, 8, LANES), f32)

        def turn(index, carry):
            adjoint, d_weight, d_decay = carry
            t = ROWS - 1 - index
            place = pl.ds(pl.multiple_of(t * TILES + half * 8, 8), 8)
            d_conv = dc_s[place, :]
            state = saved[half, t, modes]
            adjoint = adjoint * (decay * scal[t + 1]) + d_conv[None]
            mixed_grad = jnp.sum(adjoint * weight, axis=0)
            if part:
                mixed_grad = mixed_grad + dm_s[place, :]
            dm_s[place, :] = mixed_grad
            d_weight = d_weight + state * d_conv[None]
            d_decay = d_decay + adjoint * (state - mix_s[place, :][None])
            return (adjoint, d_weight, d_decay)

        _, d_weight, d_decay = lax.fori_loop(0, ROWS, turn, (zero, zero, zero))
        dw_acc[modes, rows, :] = d_weight
        de_acc[modes, rows, :] = d_decay * weight

    scan_reverse(0, 0)
    scan_reverse(0, 1)
    finish(early[0])
    own_early = aligned(spot, 16)
    e_recv[spot] = e_send[own_early, :]
    e_tot[...] = jnp.sum(e_recv[...], axis=0)
    begin(early[1])
    scan_reverse(1, 0)
    scan_reverse(1, 1)

    finish(reverse[1])
    b_zrecv[level] = b_tot[...]
    leave = jnp.zeros_like(total)
    for position in range(LEVELS - 1, 0, -1):
        longer = b_zrecv[position] + level_flag(position) * level_decay * leave
        leave = jnp.where(position > level, longer, leave)
    b_back[PLANE - 1] = leave
    for position in range(PLANE - 1, 0, -1):
        leave = b_recv[position] + plane_flag(position) * step_decay * leave
        b_back[position - 1] = leave
    begin(reverse[2])
    b_full[own_rows, :] = b_back[spot]

    finish(early[1])
    e_zrecv[level] = e_tot[...]
    e_full[own_early, :] = jnp.sum(e_zrecv[...], axis=0)
    begin(early[2])

    @pl.loop(0, TILES)
    def _(tile):
        cols = aligned(tile, LANES)
        sg2[aligned(tile, MODES), :] = per_mode(a1[:, cols], dconv16[:, cols])

    finish(reverse[2])

    @pl.loop(0, TILES)
    def _(tile):
        cols = aligned(tile, LANES)
        rows = aligned(tile, MODES)
        carried = jnp.dot(d0[:, cols], spread(b_full[rows, :]), preferred_element_type=f32)
        d_mixed = dm_s[pl.ds(tile, ROWS, stride=TILES), :] + carried
        gk[0:ROWS, cols] = d_mixed * vs_ref[:, cols]
        gv[0:ROWS, cols] = d_mixed * ks_ref[:, cols]

    k_back.start()
    v_back.start()

    @pl.loop(0, TILES)
    def _(tile):
        cols = aligned(tile, LANES)
        found = tap_rows(gk, kext, cols) + tap_rows(gv, vext, cols)
        for lag, row in enumerate(found):
            l_send[pl.ds(tile * 16 + lag, 1), :] = row

    through = plane_flag(spot) * float(ROWS)
    leaving = b_full[...]
    entering = f_full[...]
    pass_decay = jnp.exp(-lam_rows[...] * float(ROWS)) * through
    s2[...] = leaving * s2[...] + entering * (w_rows[...] * sg2[...] + leaving * pass_decay)
    sg2[...] = entering * sg0[...]
    lane_group = lax.broadcasted_iota(jnp.int32, (LANES, LANES), 0) // GROUP
    same_group = jnp.where(
        lane_group == lax.broadcasted_iota(jnp.int32, (LANES, LANES), 1) // GROUP, 1.0, 0.0
    )
    lane_mode = lax.rem(lax.broadcasted_iota(jnp.int32, (TILES, LANES), 1), MODES)

    def gather_modes(mode, carry):
        d_weight, d_decay = carry
        picked = pl.ds(mode, TILES, stride=MODES)
        chosen = lane_mode == mode
        for_weight = dw_acc[mode] + sg2[picked, :]
        for_decay = de_acc[mode] + s2[picked, :]
        both = jnp.dot(
            jnp.concatenate([for_weight, for_decay]),
            same_group,
            precision=lax.Precision.HIGHEST,
            preferred_element_type=f32,
        )
        d_weight = jnp.where(chosen, both[0:TILES], d_weight)
        d_decay = jnp.where(chosen, both[TILES : 2 * TILES], d_decay)
        return (d_weight, d_decay)

    empty = jnp.zeros((TILES, LANES), f32)
    d_weight, d_decay = lax.fori_loop(0, MODES, gather_modes, (empty, empty))
    l_send[pl.ds(14, TILES, stride=MODES), :] = d_weight
    l_send[pl.ds(15, TILES, stride=MODES), :] = d_decay
    begin(late[0])

    q_back.wait()

    @pl.loop(0, TILES)
    def _(tile):
        cols = aligned(tile, LANES)
        dq_ref[:, cols] = feature_back(gq, 0, cols)

    finish(late[0])
    l_recv[spot] = l_send[own_rows, :]
    l_tot[...] = jnp.sum(l_recv[...], axis=0)
    begin(late[1])
    k_back.wait()
    v_back.wait()

    @pl.loop(0, TILES)
    def _(tile):
        cols = aligned(tile, LANES)
        dk_ref[:, cols] = feature_back(gk, 1, cols)
        dv_ref[:, cols] = feature_back(gv, 2, cols)

    finish(early[2])
    finish(late[1])
    l_zrecv[level] = l_tot[...]
    l_full[own_rows, :] = jnp.sum(l_zrecv[...], axis=0)
    begin(late[2])

    @pl.loop(0, TILES)
    def _(tile):
        cols = aligned(tile, LANES)
        found = e_full[aligned(tile, 8), :]
        dtaps_ref[0, :, cols] = found[0:TAPS]
        dgain_ref[:, cols] = found[TAPS : TAPS + 1]

    finish(late[2])

    @pl.loop(0, TILES)
    def _(tile):
        cols = aligned(tile, LANES)
        found = l_full[aligned(tile, 16), :]
        dtaps_ref[1, :, cols] = found[0:TAPS]
        dtaps_ref[2, :, cols] = found[TAPS : 2 * TAPS]

    weight_grad = l_full[pl.ds(14, TILES, stride=MODES), :]
    dres_ref[...] = weight_grad * mode_lane[...]
    drate_ref[...] = weight_grad * rate_lane[...] - l_full[pl.ds(15, TILES, stride=MODES), :]


def on_device(
    queries, keys, values, short_taps, residues, decay_rate, out_gain, doc_lengths, upstream
):
    rows, channels = queries.shape
    me = lax.axis_index("ctx")
    starts = jnp.cumsum(doc_lengths) - doc_lengths
    positions = me * rows - EXT + jnp.arange(rows + 2 * EXT, dtype=jnp.int32)
    doc = jnp.where(positions >= TOKENS, NDOC_END, doc_index(starts, positions))
    docs = jnp.broadcast_to(doc.astype(f32)[:, None], (rows + 2 * EXT, LANES))
    same = (doc[EXT : EXT + rows + 1] == doc[EXT - 1 : EXT + rows]).astype(f32)
    ends = doc_index(starts, jnp.arange(-1, TOKENS, rows, dtype=jnp.int32))
    joins = (ends[1:] == ends[:-1]).astype(f32)
    plane_joins = lax.dynamic_slice(joins, ((me // PLANE) * PLANE,), (PLANE,))
    level_joins = (ends[PLANE::PLANE] == ends[:-1:PLANE]).astype(f32)
    scal = jnp.concatenate([same[:rows], plane_joins, level_joins])
    mode_gain = jnp.sqrt(-jnp.expm1(-2.0 * decay_rate))
    weight = residues * mode_gain
    rate_slope = residues * jnp.exp(-2.0 * decay_rate) / mode_gain

    def by_lane(per_mode):
        return per_mode.reshape(TILES, LANES)

    def by_row(per_mode):
        moved = per_mode.reshape(TILES, 8, MODES).transpose(0, 2, 1)
        return jnp.repeat(moved, GROUP, axis=2).reshape(TILES * MODES, LANES)

    any_spec = pl.BlockSpec(memory_space=pl.ANY)
    vmem = pl.BlockSpec(memory_space=pltpu.VMEM)
    wide = pltpu.VMEM((rows, channels), f32)
    wide16 = pltpu.VMEM((rows, channels), bf16)
    halo16 = pltpu.VMEM((16, channels), bf16)
    longer = pltpu.VMEM((rows + 16, channels), f32)
    scanned = pltpu.VMEM((rows * TILES, LANES), f32)
    by_modes = pltpu.VMEM((MODES, TILES, LANES), f32)
    states = pltpu.VMEM((TILES * MODES, LANES), f32)
    square = pltpu.VMEM((rows, LANES), f32)

    def pieces(chunk):
        return pltpu.VMEM((8, chunk, LANES), f32)

    def whole(chunk):
        return pltpu.VMEM((8 * chunk, LANES), f32)

    def one(chunk):
        return pltpu.VMEM((chunk, LANES), f32)

    outs = pl.pallas_call(
        kernel,
        out_shape=[
            jax.ShapeDtypeStruct((rows, channels), bf16),
            jax.ShapeDtypeStruct((rows, channels), bf16),
            jax.ShapeDtypeStruct((rows, channels), bf16),
            jax.ShapeDtypeStruct((rows, channels), bf16),
            jax.ShapeDtypeStruct((3, TAPS, channels), f32),
            jax.ShapeDtypeStruct((TILES, LANES), f32),
            jax.ShapeDtypeStruct((TILES, LANES), f32),
            jax.ShapeDtypeStruct((1, channels), f32),
        ],
        in_specs=[pl.BlockSpec(memory_space=pltpu.SMEM)] + [any_spec] * 4 + [vmem] * 8,
        out_specs=[vmem] * 8,
        scratch_shapes=[wide16] * 4
        + [halo16] * 3
        + [longer] * 3
        + [wide] * 4
        + [wide16] * 2
        + [scanned] * 4
        + [pltpu.VMEM((2, rows, MODES, 8, LANES), f32), pltpu.VMEM((TAPS, rows + EXT, LANES), f32)]
        + [wide16] * 4
        + [by_modes] * 2
        + [longer] * 3
        + [states] * 3
        + [by_modes] * 2
        + [square] * 2
        + [pltpu.VMEM((8, LANES), f32), pltpu.VMEM((CHIPS_Y, 8, LANES), f32)]
        + [whole(32), pieces(32), one(32), pieces(32), pieces(32), whole(32)] * 2
        + [whole(16), pieces(16), one(16), pieces(16), whole(16)]
        + [whole(32), pieces(32), one(32), pieces(32), whole(32)]
        + [
            pltpu.SemaphoreType.DMA((4,)),
            pltpu.SemaphoreType.DMA((6,)),
            pltpu.SemaphoreType.DMA((6,)),
            pltpu.SemaphoreType.DMA((CHIPS_Y,)),
            pltpu.SemaphoreType.DMA((CHIPS_Y,)),
            pltpu.SemaphoreType.DMA((12, 8)),
            pltpu.SemaphoreType.DMA((12, 8)),
        ],
        compiler_params=pltpu.CompilerParams(
            collective_id=0, has_side_effects=True, vmem_limit_bytes=60 * 1024 * 1024
        ),
        name="mixer",
    )(
        scal,
        queries,
        keys,
        values,
        upstream,
        short_taps,
        out_gain.reshape(1, channels),
        docs,
        by_lane(decay_rate),
        by_lane(mode_gain),
        by_lane(rate_slope),
        by_row(decay_rate),
        by_row(weight),
    )
    mixed_out, d_queries, d_keys, d_values, d_taps, d_residues, d_rate, d_gain = outs
    groups = channels // GROUP
    return (
        mixed_out,
        d_queries,
        d_keys,
        d_values,
        d_taps,
        d_residues.reshape(groups, MODES),
        d_rate.reshape(groups, MODES),
        d_gain.reshape(channels),
    )


NDOC_END = 1 << 10


def solution(mesh):
    placed = (
        P("ctx", "ch"),
        P("ctx", "ch"),
        P("ctx", "ch"),
        P(None, None, "ch"),
        P("ch", None),
        P("ch", None),
        P("ch"),
        P(),
        P("ctx", "ch"),
    )
    return jax.shard_map(
        on_device,
        mesh=mesh,
        in_specs=placed,
        out_specs=(
            P("ctx", "ch"),
            P("ctx", "ch"),
            P("ctx", "ch"),
            P("ctx", "ch"),
            P(None, None, "ch"),
            P("ch", None),
            P("ch", None),
            P("ch"),
        ),
        check_vma=False,
    )
```

```python
import functools

import jax
import jax.numpy as jnp
from jax import lax
from jax.experimental import pallas as pl
from jax.experimental.pallas import tpu as pltpu
from jax.sharding import PartitionSpec as P

D = 8192
TOKENS = 8192
GROUP = 16
MODES = 16
TAPS = 7
ROWS = 128
LANES = 128
TILES = 16
PLANE = 8
LEVELS = 8
CHIPS_Y = 4
NDOC = 16
UNROLL = 4
EXT = 8
epsilon = 1e-06
f32 = jnp.float32
bf16 = jnp.bfloat16
MESH = pl.DeviceIdType.MESH


def aligned(index, size):
    return pl.ds(pl.multiple_of(index * size, size), size)


def kernel(
    docs_hbm,
    q_hbm,
    k_hbm,
    v_hbm,
    u_hbm,
    taps_hbm,
    gain_hbm,
    res_hbm,
    rate_hbm,
    out_hbm,
    dq_hbm,
    dk_hbm,
    dv_hbm,
    dtaps_hbm,
    dres_hbm,
    drate_hbm,
    dgain_hbm,
    lengths,
    taps,
    gain,
    res,
    rate,
    out_ref,
    dq_ref,
    dk_ref,
    dv_ref,
    dtaps_ref,
    dres_ref,
    drate_ref,
    dgain_ref,
    qbuf,
    kbuf,
    vbuf,
    ubuf,
    qhalo,
    khalo,
    vhalo,
    qext,
    kext,
    vext,
    qs_ref,
    ks_ref,
    vs_ref,
    conv_ref,
    mix16,
    dconv16,
    mix_s,
    win_s,
    dc_s,
    dm_s,
    saved,
    mask,
    docs,
    ends,
    flags,
    a0,
    a1,
    d0,
    d1,
    e_n,
    w_n,
    lam_rows,
    w_rows,
    pass_rows,
    gq,
    gk,
    gv,
    sg0,
    s2,
    sg2,
    dw_acc,
    de_acc,
    part_a,
    part_b,
    sums_t,
    ysend,
    yrecv,
    f_send,
    f_recv,
    f_tot,
    f_zrecv,
    f_back,
    f_full,
    b_send,
    b_recv,
    b_tot,
    b_zrecv,
    b_back,
    b_full,
    e_send,
    e_recv,
    e_tot,
    e_zrecv,
    e_full,
    l_send,
    l_recv,
    l_tot,
    l_zrecv,
    l_full,
    load_sem,
    store_sem,
    halo_s,
    halo_r,
    y_s,
    y_r,
    send_sem,
    recv_sem,
):
    me = lax.axis_index("ctx")
    cy = lax.axis_index("ch")
    level = me // PLANE
    spot = lax.rem(me, PLANE)
    nodes = PLANE * LEVELS
    after = lax.rem(me + 1, nodes)
    before = lax.rem(me + nodes - 1, nodes)

    def in_plane(step):
        return lax.rem(spot + step, PLANE)

    def on_level(step):
        return lax.rem(level + step, LEVELS)

    barrier = pltpu.get_barrier_semaphore()
    for step in range(1, PLANE):
        pl.semaphore_signal(
            barrier, inc=1, device_id={"ctx": level * PLANE + in_plane(step)}, device_id_type=MESH
        )
    for step in range(1, LEVELS):
        pl.semaphore_signal(
            barrier, inc=1, device_id={"ctx": on_level(step) * PLANE + spot}, device_id_type=MESH
        )
    for step in range(1, CHIPS_Y):
        pl.semaphore_signal(
            barrier, inc=1, device_id={"ch": lax.rem(cy + step, CHIPS_Y)}, device_id_type=MESH
        )
    for other in (before, after):
        pl.semaphore_signal(barrier, inc=1, device_id={"ctx": other}, device_id_type=MESH)

    small = [
        pltpu.make_async_copy(source, target, load_sem.at[4 + i])
        for i, (source, target) in enumerate(
            (
                (docs_hbm, lengths),
                (rate_hbm, rate),
                (res_hbm, res),
                (taps_hbm, taps),
                (gain_hbm, gain),
            )
        )
    ]
    loads = [
        pltpu.make_async_copy(source, target, load_sem.at[i])
        for i, (source, target) in enumerate(
            ((k_hbm, kbuf), (v_hbm, vbuf), (q_hbm, qbuf), (u_hbm, ubuf))
        )
    ]
    for load in small + loads:
        load.start()

    small[0].wait()
    starts = [0]
    for i in range(NDOC - 1):
        starts.append(starts[-1] + lengths[i])

    def doc_of(positions):
        found = jnp.zeros_like(positions) - 1
        for start in starts:
            found = found + jnp.where(positions >= start, 1, 0)
        return found

    place = lax.broadcasted_iota(jnp.int32, (ROWS + 2 * EXT, LANES), 0) + (me * ROWS - EXT)
    docs[...] = jnp.where(place >= TOKENS, NDOC, doc_of(place))
    block = lax.broadcasted_iota(jnp.int32, (24, LANES), 0)
    block = jnp.where(block < 12, level * PLANE + block, (block - 12) * PLANE)
    ends[...] = doc_of(block * ROWS - 1)
    flags[0:8] = jnp.where(ends[0:8, :] == ends[1:9, :], 1.0, 0.0)
    flags[8:16] = jnp.where(ends[12:20, :] == ends[13:21, :], 1.0, 0.0)

    here = docs[EXT : EXT + ROWS + EXT, :]
    for lag in range(1, TAPS):
        same = docs[EXT - lag : EXT - lag + ROWS + EXT, :] == here
        mask[lag] = jnp.where(same, 1.0, 0.0)
    part_a[...] = jnp.where(docs[EXT : EXT + ROWS, :] == docs[EXT - 1 : EXT, :], 1.0, 0.0)
    part_b[...] = jnp.where(
        docs[EXT : EXT + ROWS, :] == docs[EXT + ROWS - 1 : EXT + ROWS, :], 1.0, 0.0
    )
    row_number = lax.broadcasted_iota(jnp.int32, (ROWS, LANES), 0).astype(f32)
    on_group = lax.broadcasted_iota(jnp.int32, (8, MODES, LANES), 0) == (
        lax.broadcasted_iota(jnp.int32, (8, MODES, LANES), 2) // GROUP
    )
    own_mode = lax.broadcasted_iota(jnp.int32, (MODES, LANES), 0) == (
        lax.rem(lax.broadcasted_iota(jnp.int32, (MODES, LANES), 1), MODES)
    )
    near = lax.broadcasted_iota(jnp.int32, (LANES, LANES), 0) - (
        lax.broadcasted_iota(jnp.int32, (LANES, LANES), 1) // GROUP
    )
    far = lax.broadcasted_iota(jnp.int32, (LANES, LANES), 1) - (
        lax.broadcasted_iota(jnp.int32, (LANES, LANES), 0) // GROUP
    )
    small[1].wait()
    small[2].wait()
    twice = 2.0 * rate[...]
    series = 1.0 - twice / 6.0
    for term in (5.0, 4.0, 3.0, 2.0):
        series = 1.0 - (twice / term) * series
    mode_gain = jnp.sqrt(jnp.where(twice < 0.125, twice * series, 1.0 - jnp.exp(-twice)))
    both = jnp.concatenate([rate[...], res[...] * mode_gain])

    @pl.loop(0, TILES)
    def _(tile):
        cols = aligned(tile, LANES)
        rows = aligned(tile, MODES)
        widened = jnp.dot(
            both,
            jnp.where(near == tile * 8, 1.0, 0.0),
            precision=lax.Precision.HIGHEST,
            preferred_element_type=f32,
        )
        rates = widened[0:MODES]
        lam_rows[rows, :] = rates
        w_rows[rows, :] = widened[MODES : 2 * MODES]
        pass_rows[rows, :] = jnp.exp(-rates * float(ROWS))
        lam = jnp.sum(jnp.where(own_mode, rates, 0.0), axis=0, keepdims=True)
        ahead = jnp.exp(-lam * (row_number + 1.0)) * part_a[...]
        behind = jnp.exp(-lam * (ROWS - 1.0 - row_number)) * part_b[...]
        a0[:, cols] = ahead.astype(bf16)
        d0[:, cols] = behind.astype(bf16)
        a1[:, cols] = (ahead * (row_number + 1.0)).astype(bf16)
        d1[:, cols] = (behind * (ROWS - 1.0 - row_number)).astype(bf16)

    small[3].wait()
    small[4].wait()
    pl.semaphore_wait(barrier, PLANE - 1 + LEVELS - 1 + CHIPS_Y - 1 + 2)

    halos = [
        pltpu.make_async_remote_copy(
            src_ref=source.at[pl.ds(ROWS - EXT, EXT)],
            dst_ref=target,
            send_sem=halo_s.at[i],
            recv_sem=halo_r.at[i],
            device_id={"ctx": after},
            device_id_type=MESH,
        )
        for i, (source, target) in enumerate(((k_hbm, khalo), (v_hbm, vhalo), (q_hbm, qhalo)))
    ]
    for halo in halos:
        halo.start()

    def feature(ext, which, cols, begin, end):
        total = taps[which, 0:1, cols] * ext[EXT + begin : EXT + end, cols]
        for lag in range(1, TAPS):
            shifted = ext[EXT + begin - lag : EXT + end - lag, cols] * mask[lag, begin:end, :]
            total = total + taps[which, lag : lag + 1, cols] * shifted
        return total

    def per_mode(left, right):
        blocks = lax.dot_general(left, right, (((0,), (0,)), ((), ())), preferred_element_type=f32)
        return jnp.sum(jnp.where(on_group, blocks.reshape(8, MODES, LANES), 0.0), axis=0)

    def spread(state):
        wide = jnp.broadcast_to(state[None], (8, MODES, LANES))
        return jnp.where(on_group, wide, 0.0).reshape(8 * MODES, LANES).astype(bf16)

    def plane_copies(base, source, target, chunk):
        out, back = [], []
        for step in range(1, PLANE):
            other = in_plane(step)
            device = level * PLANE + other
            src = source(other)
            out.append(
                pltpu.make_async_remote_copy(
                    src_ref=src,
                    dst_ref=target(spot),
                    send_sem=send_sem.at[base, other],
                    recv_sem=recv_sem.at[base, spot],
                    device_id={"ctx": device},
                    device_id_type=MESH,
                )
            )
            back.append(
                pltpu.make_async_remote_copy(
                    src_ref=src,
                    dst_ref=target(other),
                    send_sem=send_sem.at[base, other],
                    recv_sem=recv_sem.at[base, other],
                    device_id={"ctx": device},
                    device_id_type=MESH,
                )
            )
        return out, back

    def level_copies(base, source, target):
        out, back = [], []
        for step in range(1, LEVELS):
            other = on_level(step)
            device = other * PLANE + spot
            for kept, slot in ((out, level), (back, other)):
                kept.append(
                    pltpu.make_async_remote_copy(
                        src_ref=source,
                        dst_ref=target.at[slot],
                        send_sem=send_sem.at[base, other],
                        recv_sem=recv_sem.at[base, slot],
                        device_id={"ctx": device},
                        device_id_type=MESH,
                    )
                )
        return out, back

    def begin(copies):
        for copy in copies[0]:
            copy.start()

    def finish(copies):
        for copy in copies[1]:
            copy.wait()

    def send_chunk(base, send, recv, other, chunk):
        pltpu.make_async_remote_copy(
            src_ref=send.at[aligned(other, chunk)],
            dst_ref=recv.at[spot],
            send_sem=send_sem.at[base, other],
            recv_sem=recv_sem.at[base, spot],
            device_id={"ctx": level * PLANE + other},
            device_id_type=MESH,
        ).start()

    def by_chunks(work, base, send, recv):
        @pl.loop(0, PLANE)
        def _(turn):
            chunk = lax.rem(spot + 1 + turn, PLANE)

            @pl.loop(0, 2)
            def _(part):
                work(chunk * 2 + part)

            @pl.when(turn < PLANE - 1)
            def _():
                send_chunk(base, send, recv, chunk, 32)

    def exchange(base, send, recv, tot, zrecv, back, full, chunk):
        first = plane_copies(base, lambda o: send.at[aligned(o, chunk)], lambda s: recv.at[s], chunk)
        second = level_copies(base + 1, tot, zrecv)
        if back is None:
            third = plane_copies(
                base + 2,
                lambda o: full.at[aligned(spot, chunk)],
                lambda s: full.at[aligned(s, chunk)],
                chunk,
            )
        else:
            third = plane_copies(
                base + 2, lambda o: back.at[o], lambda s: full.at[aligned(s, chunk)], chunk
            )
        return first, second, third

    forward = exchange(0, f_send, f_recv, f_tot, f_zrecv, f_back, f_full, 32)
    reverse = exchange(3, b_send, b_recv, b_tot, b_zrecv, b_back, b_full, 32)
    early = exchange(6, e_send, e_recv, e_tot, e_zrecv, None, e_full, 16)
    late = exchange(9, l_send, l_recv, l_tot, l_zrecv, None, l_full, 32)

    own_rows = aligned(spot, 32)

    def plane_flag(position):
        return flags[position : position + 1, :]

    def level_flag(position):
        return flags[8 + position : 9 + position, :]

    def emit(ref, hbm, index):
        copy = pltpu.make_async_copy(ref, hbm, store_sem.at[index])
        copy.start()
        return copy

    loads[0].wait()
    loads[1].wait()

    @pl.loop(0, TILES)
    def _(tile):
        cols = aligned(tile, LANES)
        kext[EXT : EXT + ROWS, cols] = kbuf[:, cols].astype(f32)
        vext[EXT : EXT + ROWS, cols] = vbuf[:, cols].astype(f32)
        for begin_row, end_row in ((16, 48), (48, 80), (80, 112), (112, 128)):
            ks = feature(kext, 1, cols, begin_row, end_row)
            vs = feature(vext, 2, cols, begin_row, end_row)
            mixed = ks * vs
            ks_ref[begin_row:end_row, cols] = ks
            vs_ref[begin_row:end_row, cols] = vs
            mix_s[pl.ds(begin_row * TILES + tile, end_row - begin_row, stride=TILES), :] = mixed
            mix16[begin_row:end_row, cols] = mixed.astype(bf16)

    halos[0].wait()
    halos[1].wait()

    def end_state(tile):
        cols = aligned(tile, LANES)
        kext[0:EXT, cols] = khalo[:, cols].astype(f32)
        vext[0:EXT, cols] = vhalo[:, cols].astype(f32)
        ks = feature(kext, 1, cols, 0, 16)
        vs = feature(vext, 2, cols, 0, 16)
        mixed = ks * vs
        ks_ref[0:16, cols] = ks
        vs_ref[0:16, cols] = vs
        mix_s[pl.ds(tile, 16, stride=TILES), :] = mixed
        mix16[0:16, cols] = mixed.astype(bf16)
        f_send[aligned(tile, MODES), :] = per_mode(d0[:, cols], mix16[:, cols])

    by_chunks(end_state, 0, f_send, f_recv)
    loads[2].wait()
    halos[2].wait()

    @pl.loop(0, TILES)
    def _(tile):
        cols = aligned(tile, LANES)
        qext[EXT : EXT + ROWS, cols] = qbuf[:, cols].astype(f32)
        qext[0:EXT, cols] = qhalo[:, cols].astype(f32)
        for begin_row in range(0, ROWS, 32):
            qs_ref[begin_row : begin_row + 32, cols] = feature(
                qext, 0, cols, begin_row, begin_row + 32
            )

    @pl.loop(0, MODES)
    def _(mode):
        e_n[mode] = jnp.exp(-lam_rows[pl.ds(mode, TILES, stride=MODES), :])
        w_n[mode] = w_rows[pl.ds(mode, TILES, stride=MODES), :]

    step_decay = jnp.exp(-lam_rows[own_rows, :] * float(ROWS))
    level_decay = jnp.exp(-lam_rows[own_rows, :] * float(ROWS * PLANE))

    finish(forward[0])
    f_recv[spot] = f_send[own_rows, :]
    total = f_recv[0]
    for position in range(1, PLANE):
        total = plane_flag(position) * (step_decay * total) + f_recv[position]
    f_tot[...] = total.astype(bf16)
    begin(forward[1])

    def scan_forward(half):
        rows = slice(half * 8, half * 8 + 8)
        decay = e_n[:, rows, :]
        weight = w_n[:, rows, :]

        def turn(t, state):
            place = pl.ds(pl.multiple_of(t * TILES + half * 8, 8), 8)
            state = state * (decay * mask[1, pl.ds(t, 1), :][None]) + mix_s[place, :][None]
            saved[half, t] = state
            win_s[place, :] = jnp.sum(state * weight, axis=0)
            return state

        lax.fori_loop(0, ROWS, turn, jnp.zeros((MODES, 8, LANES), f32), unroll=UNROLL)

    scan_forward(0)
    scan_forward(1)

    finish(forward[1])
    f_zrecv[level] = f_tot[...]
    enter = jnp.zeros_like(total)
    for position in range(LEVELS - 1):
        longer = level_flag(position) * (level_decay * enter) + f_zrecv[position].astype(f32)
        enter = jnp.where(position < level, longer, enter)
    f_back[0] = enter.astype(bf16)
    for position in range(PLANE - 1):
        enter = plane_flag(position) * (step_decay * enter) + f_recv[position]
        f_back[position + 1] = enter.astype(bf16)
    begin(forward[2])
    f_full[own_rows, :] = f_back[spot]

    @pl.loop(0, TILES)
    def _(tile):
        cols = aligned(tile, LANES)
        s2[aligned(tile, MODES), :] = per_mode(d1[:, cols], mix16[:, cols])

    finish(forward[2])
    loads[3].wait()

    part_a[...] = jnp.zeros_like(part_a)
    part_b[...] = jnp.zeros_like(part_b)

    @pl.loop(0, TILES)
    def _(tile):
        cols = aligned(tile, LANES)
        rows = aligned(tile, MODES)
        carried = jnp.dot(
            a0[:, cols], spread(f_full[rows, :].astype(f32) * w_rows[rows, :]), preferred_element_type=f32
        )
        conv = win_s[pl.ds(tile, ROWS, stride=TILES), :] + carried
        conv_ref[:, cols] = conv
        gated = qs_ref[:, cols] * conv
        part_a[...] += gated * gated
        part_b[...] += ubuf[:, cols].astype(f32) * gain[pl.ds(tile, 1), :] * gated

    squares = jnp.sum(part_a[...].T, axis=0, keepdims=True)
    inner = jnp.sum(part_b[...].T, axis=0, keepdims=True)
    upper = lax.broadcasted_iota(jnp.int32, (8, LANES), 0) == 0
    ysend[...] = jnp.where(
        upper, jnp.broadcast_to(squares, (8, LANES)), jnp.broadcast_to(inner, (8, LANES))
    )
    y_out, y_back = [], []
    for step in range(1, CHIPS_Y):
        other = lax.rem(cy + step, CHIPS_Y)
        for kept, slot in ((y_out, cy), (y_back, other)):
            kept.append(
                pltpu.make_async_remote_copy(
                    src_ref=ysend,
                    dst_ref=yrecv.at[slot],
                    send_sem=y_s.at[other],
                    recv_sem=y_r.at[slot],
                    device_id={"ch": other},
                    device_id_type=MESH,
                )
            )
    begin((y_out, y_back))
    finish((y_out, y_back))
    yrecv[cy] = ysend[...]
    sums = yrecv[0] + yrecv[1] + yrecv[2] + yrecv[3]
    inv_row = lax.rsqrt(sums[0:1] / D + epsilon)
    pull_row = inv_row * inv_row * inv_row * sums[1:2] / D
    part_a[...] = jnp.broadcast_to(inv_row, (ROWS, LANES)).T
    part_b[...] = jnp.broadcast_to(pull_row, (ROWS, LANES)).T

    def output_grad(tile):
        cols = aligned(tile, LANES)
        rows = aligned(tile, MODES)
        qs = qs_ref[:, cols]
        conv = conv_ref[:, cols]
        inverse = part_a[...]
        up = ubuf[:, cols].astype(f32)
        scale = gain[pl.ds(tile, 1), :]
        gated = qs * conv
        d_gated = inverse * (up * scale) - gated * part_b[...]
        normed = gated * inverse
        d_conv = d_gated * qs
        out_ref[:, cols] = (normed * scale).astype(bf16)
        gq[0:ROWS, cols] = d_gated * conv
        dc_s[pl.ds(tile, ROWS, stride=TILES), :] = d_conv
        dconv16[:, cols] = d_conv.astype(bf16)
        local = per_mode(a0[:, cols], d_conv.astype(bf16))
        sg0[rows, :] = local
        b_send[rows, :] = local * w_rows[rows, :]
        e_send[pl.ds(tile * 8 + 7, 1), :] = jnp.sum(up * normed, axis=0, keepdims=True)

    by_chunks(output_grad, 3, b_send, b_recv)
    stores = [emit(out_ref, out_hbm, 0)]

    def halo_back(index, ref):
        return pltpu.make_async_remote_copy(
            src_ref=ref.at[pl.ds(0, 8)],
            dst_ref=ref.at[pl.ds(ROWS, 8)],
            send_sem=halo_s.at[3 + index],
            recv_sem=halo_r.at[3 + index],
            device_id={"ctx": before},
            device_id_type=MESH,
        )

    q_back, k_back, v_back = halo_back(0, gq), halo_back(1, gk), halo_back(2, gv)
    q_back.start()

    def tap_rows(grad, ext, cols):
        rows = []
        here = grad[0:ROWS, cols]
        for lag in range(TAPS):
            product = here * ext[EXT - lag : EXT - lag + ROWS, cols]
            if lag:
                product = product * mask[lag, 0:ROWS, :]
            rows.append(jnp.sum(product, axis=0, keepdims=True))
        return rows

    def feature_back(grad, which, cols):
        total = taps[which, 0:1, cols] * grad[0:ROWS, cols]
        for lag in range(1, TAPS):
            shifted = grad[lag : lag + ROWS, cols] * mask[lag, lag : lag + ROWS, :]
            total = total + taps[which, lag : lag + 1, cols] * shifted
        return total.astype(bf16)

    @pl.loop(0, TILES)
    def _(tile):
        cols = aligned(tile, LANES)
        for lag, row in enumerate(tap_rows(gq, qext, cols)):
            e_send[pl.ds(tile * 8 + lag, 1), :] = row

    begin(early[0])

    finish(reverse[0])
    b_recv[spot] = b_send[own_rows, :]
    total = b_recv[PLANE - 1]
    for position in range(PLANE - 2, -1, -1):
        total = b_recv[position] + plane_flag(position) * (step_decay * total)
    b_tot[...] = total.astype(bf16)
    begin(reverse[1])

    def scan_reverse(half, part):
        rows = slice(half * 8, half * 8 + 8)
        modes = slice(part * 8, part * 8 + 8)
        decay = e_n[modes, rows, :]
        weight = w_n[modes, rows, :]
        zero = jnp.zeros((8, 8, LANES), f32)

        def turn(index, carry):
            adjoint, d_weight, d_decay = carry
            t = ROWS - 1 - index
            place = pl.ds(pl.multiple_of(t * TILES + half * 8, 8), 8)
            d_conv = dc_s[place, :]
            state = saved[half, t, modes]
            adjoint = adjoint * (decay * mask[1, pl.ds(t + 1, 1), :][None]) + d_conv[None]
            mixed_grad = jnp.sum(adjoint * weight, axis=0)
            if part:
                mixed_grad = mixed_grad + dm_s[place, :]
            dm_s[place, :] = mixed_grad
            d_weight = d_weight + state * d_conv[None]
            d_decay = d_decay + adjoint * (state - mix_s[place, :][None])
            return (adjoint, d_weight, d_decay)

        _, d_weight, d_decay = lax.fori_loop(0, ROWS, turn, (zero, zero, zero), unroll=UNROLL)
        for mode in range(8):
            slot = slice((part * 8 + mode) * TILES + half * 8, (part * 8 + mode) * TILES + half * 8 + 8)
            dw_acc[slot, :] = d_weight[mode]
            de_acc[slot, :] = d_decay[mode] * weight[mode]

    scan_reverse(0, 0)
    scan_reverse(0, 1)
    finish(early[0])
    own_early = aligned(spot, 16)
    e_recv[spot] = e_send[own_early, :]
    e_tot[...] = jnp.sum(e_recv[...], axis=0).astype(bf16)
    begin(early[1])
    scan_reverse(1, 0)
    scan_reverse(1, 1)

    finish(reverse[1])
    b_zrecv[level] = b_tot[...]
    leave = jnp.zeros_like(total)
    for position in range(LEVELS - 1, 0, -1):
        longer = b_zrecv[position].astype(f32) + level_flag(position) * (level_decay * leave)
        leave = jnp.where(position > level, longer, leave)
    b_back[PLANE - 1] = leave.astype(bf16)
    for position in range(PLANE - 1, 0, -1):
        leave = b_recv[position] + plane_flag(position) * (step_decay * leave)
        b_back[position - 1] = leave.astype(bf16)
    begin(reverse[2])
    b_full[own_rows, :] = b_back[spot]

    finish(early[1])
    e_zrecv[level] = e_tot[...]
    e_full[own_early, :] = jnp.sum(e_zrecv[...].astype(f32), axis=0)
    begin(early[2])

    through = flags[pl.ds(spot, 1), :] * float(ROWS)

    def exact_dot(value, chosen):
        high = value.astype(bf16)
        low = (value - high.astype(f32)).astype(bf16)
        stacked = jnp.dot(
            jnp.concatenate([high, low]), chosen, preferred_element_type=f32
        )
        return stacked[0 : value.shape[0]] + stacked[value.shape[0] :]

    def local_modes(tile, carry):
        cols = aligned(tile, LANES)
        rows = aligned(tile, MODES)
        chosen = jnp.where(far == tile * 8, 1.0, 0.0).astype(bf16)
        entering = f_full[rows, :].astype(f32)
        picked = pl.ds(tile, MODES, stride=TILES)
        second = per_mode(a1[:, cols], dconv16[:, cols])
        for_weight = dw_acc[picked, :] + entering * sg0[rows, :]
        for_decay = de_acc[picked, :] + entering * (w_rows[rows, :] * second)
        s2[rows, :] = s2[rows, :] + entering * (pass_rows[rows, :] * through)
        return carry + exact_dot(jnp.concatenate([for_weight, for_decay]), chosen)

    mode_grads = lax.fori_loop(0, TILES, local_modes, jnp.zeros((2 * MODES, LANES), f32))
    q_back.wait()

    @pl.loop(0, TILES)
    def _(tile):
        cols = aligned(tile, LANES)
        dq_ref[:, cols] = feature_back(gq, 0, cols)

    stores.append(emit(dq_ref, dq_hbm, 1))
    finish(reverse[2])

    def leaving_modes(tile, carry):
        rows = aligned(tile, MODES)
        chosen = jnp.where(far == tile * 8, 1.0, 0.0).astype(bf16)
        return carry + exact_dot(b_full[rows, :].astype(f32) * s2[rows, :], chosen)

    decay_grad = mode_grads[MODES:] + lax.fori_loop(
        0, TILES, leaving_modes, jnp.zeros((MODES, LANES), f32)
    )
    l_send[pl.ds(14, TILES, stride=MODES), :] = mode_grads[:MODES]
    l_send[pl.ds(15, TILES, stride=MODES), :] = decay_grad

    def featurizer_grad(tile):
        cols = aligned(tile, LANES)
        rows = aligned(tile, MODES)
        carried = jnp.dot(d0[:, cols], spread(b_full[rows, :]), preferred_element_type=f32)
        d_mixed = dm_s[pl.ds(tile, ROWS, stride=TILES), :] + carried
        gk[0:ROWS, cols] = d_mixed * vs_ref[:, cols]
        gv[0:ROWS, cols] = d_mixed * ks_ref[:, cols]
        found = tap_rows(gk, kext, cols) + tap_rows(gv, vext, cols)
        for lag, row in enumerate(found):
            l_send[pl.ds(tile * 16 + lag, 1), :] = row

    by_chunks(featurizer_grad, 9, l_send, l_recv)
    k_back.start()
    v_back.start()
    finish(early[2])

    @pl.loop(0, TILES)
    def _(tile):
        cols = aligned(tile, LANES)
        dtaps_ref[0, :, cols] = e_full[aligned(tile, 8), :][0:TAPS]

    dgain_ref[...] = e_full[pl.ds(7, TILES, stride=8), :]
    stores.append(emit(dgain_ref, dgain_hbm, 2))

    finish(late[0])
    l_recv[spot] = l_send[own_rows, :]
    l_tot[...] = jnp.sum(l_recv[...], axis=0).astype(bf16)
    begin(late[1])
    k_back.wait()
    v_back.wait()

    @pl.loop(0, TILES)
    def _(tile):
        cols = aligned(tile, LANES)
        dk_ref[:, cols] = feature_back(gk, 1, cols)
        dv_ref[:, cols] = feature_back(gv, 2, cols)

    finish(late[1])
    l_zrecv[level] = l_tot[...]
    l_full[own_rows, :] = jnp.sum(l_zrecv[...].astype(f32), axis=0)
    begin(late[2])
    stores.append(emit(dk_ref, dk_hbm, 3))
    stores.append(emit(dv_ref, dv_hbm, 4))
    finish(late[2])

    @pl.loop(0, TILES)
    def _(tile):
        cols = aligned(tile, LANES)
        found = l_full[aligned(tile, 16), :]
        dtaps_ref[1, :, cols] = found[0:TAPS]
        dtaps_ref[2, :, cols] = found[TAPS : 2 * TAPS]

    stores.append(emit(dtaps_ref, dtaps_hbm, 5))
    weight_grad = l_full[pl.ds(14, TILES, stride=MODES), :]
    dres_ref[...] = weight_grad * mode_gain
    drate_ref[...] = (
        weight_grad * (res[...] * jnp.exp(-twice) / mode_gain)
        - l_full[pl.ds(15, TILES, stride=MODES), :]
    )
    stores.append(emit(dres_ref, dres_hbm, 6))
    stores.append(emit(drate_ref, drate_hbm, 7))
    for store in stores:
        store.wait()


def hand_over(*refs):
    count = (len(refs) - 2) // 3
    sources, targets, held = refs[:count], refs[count : 2 * count], refs[2 * count : 3 * count]
    in_sem, out_sem = refs[-2:]
    inward = [
        pltpu.make_async_copy(sources[i], held[i], in_sem.at[i]) for i in range(count)
    ]
    outward = [
        pltpu.make_async_copy(held[i], targets[i], out_sem.at[i]) for i in range(count)
    ]
    for copy in inward:
        copy.start()
    for i in range(count):
        inward[i].wait()
        outward[i].start()
    for copy in outward:
        copy.wait()


def on_device(
    queries, keys, values, short_taps, residues, decay_rate, out_gain, doc_lengths, upstream
):
    rows, channels = queries.shape
    any_spec = pl.BlockSpec(memory_space=pl.ANY)
    wide = pltpu.VMEM((rows, channels), f32)
    wide16 = pltpu.VMEM((rows, channels), bf16)
    halo16 = pltpu.VMEM((EXT, channels), bf16)
    longer = pltpu.VMEM((rows + 16, channels), f32)
    scanned = pltpu.VMEM((rows * TILES, LANES), f32)
    by_modes = pltpu.VMEM((MODES, TILES, LANES), f32)
    small = pltpu.VMEM((TILES, LANES), f32)
    states = pltpu.VMEM((TILES * MODES, LANES), f32)
    square = pltpu.VMEM((rows, LANES), f32)

    def pieces(chunk, kind=f32):
        return pltpu.VMEM((8, chunk, LANES), kind)

    def whole(chunk, kind=f32):
        return pltpu.VMEM((8 * chunk, LANES), kind)

    def one(chunk, kind=bf16):
        return pltpu.VMEM((chunk, LANES), kind)

    shapes = [
        jax.ShapeDtypeStruct((rows, channels), bf16),
        jax.ShapeDtypeStruct((rows, channels), bf16),
        jax.ShapeDtypeStruct((rows, channels), bf16),
        jax.ShapeDtypeStruct((rows, channels), bf16),
        jax.ShapeDtypeStruct((3, TAPS, channels), f32),
        jax.ShapeDtypeStruct((TILES, LANES), f32),
        jax.ShapeDtypeStruct((TILES, LANES), f32),
        jax.ShapeDtypeStruct((TILES, LANES), f32),
    ]
    held = [pltpu.VMEM(shape.shape, shape.dtype) for shape in shapes]
    outs = pl.pallas_call(
        kernel,
        out_shape=shapes,
        in_specs=[any_spec] * 9,
        out_specs=[any_spec] * 8,
        scratch_shapes=[
            pltpu.SMEM((NDOC,), jnp.int32),
            pltpu.VMEM((3, TAPS, channels), f32),
            small,
            small,
            small,
        ]
        + held
        + [wide16] * 4
        + [halo16] * 3
        + [longer] * 3
        + [wide] * 4
        + [wide16] * 2
        + [scanned] * 4
        + [
            pltpu.VMEM((2, rows, MODES, 8, LANES), f32),
            pltpu.VMEM((TAPS, rows + EXT, LANES), f32),
            pltpu.VMEM((rows + 2 * EXT, LANES), jnp.int32),
            pltpu.VMEM((24, LANES), jnp.int32),
            small,
        ]
        + [wide16] * 4
        + [by_modes] * 2
        + [states] * 3
        + [longer] * 3
        + [states] * 3
        + [states] * 2
        + [square] * 2
        + [square] + [pltpu.VMEM((8, LANES), f32), pltpu.VMEM((CHIPS_Y, 8, LANES), f32)]
        + [whole(32), pieces(32), one(32), pieces(32, bf16), pieces(32, bf16), whole(32, bf16)] * 2
        + [whole(16), pieces(16), one(16), pieces(16, bf16), whole(16)]
        + [whole(32), pieces(32), one(32), pieces(32, bf16), whole(32)]
        + [
            pltpu.SemaphoreType.DMA((9,)),
            pltpu.SemaphoreType.DMA((8,)),
            pltpu.SemaphoreType.DMA((6,)),
            pltpu.SemaphoreType.DMA((6,)),
            pltpu.SemaphoreType.DMA((CHIPS_Y,)),
            pltpu.SemaphoreType.DMA((CHIPS_Y,)),
            pltpu.SemaphoreType.DMA((12, 8)),
            pltpu.SemaphoreType.DMA((12, 8)),
        ],
        compiler_params=pltpu.CompilerParams(
            collective_id=0, has_side_effects=True, vmem_limit_bytes=60 * 1024 * 1024
        ),
        name="mixer",
    )(
        doc_lengths,
        queries,
        keys,
        values,
        upstream,
        short_taps,
        out_gain.reshape(TILES, LANES),
        residues.T,
        decay_rate.T,
    )
    outs = pl.pallas_call(
        hand_over,
        out_shape=shapes,
        in_specs=[any_spec] * 8,
        out_specs=[any_spec] * 8,
        scratch_shapes=held + [pltpu.SemaphoreType.DMA((8,)), pltpu.SemaphoreType.DMA((8,))],
        name="hand_over",
    )(*outs)
    mixed_out, d_queries, d_keys, d_values, d_taps, d_residues, d_rate, d_gain = outs
    return (
        mixed_out,
        d_queries,
        d_keys,
        d_values,
        d_taps,
        d_residues.T,
        d_rate.T,
        d_gain.reshape(channels),
    )


def solution(mesh):
    placed = (
        P("ctx", "ch"),
        P("ctx", "ch"),
        P("ctx", "ch"),
        P(None, None, "ch"),
        P("ch", None),
        P("ch", None),
        P("ch"),
        P(),
        P("ctx", "ch"),
    )
    return jax.shard_map(
        on_device,
        mesh=mesh,
        in_specs=placed,
        out_specs=(
            P("ctx", "ch"),
            P("ctx", "ch"),
            P("ctx", "ch"),
            P("ctx", "ch"),
            P(None, None, "ch"),
            P("ch", None),
            P("ch", None),
            P("ch"),
        ),
        check_vma=False,
    )
```
